32 devices in a mesh: group: 2 (over y), tile: 4 (over z), list: 4 (over x, core).
Axes of the slice: x: 2, y: 2, z: 4, core: 2. Of those that a mesh axis runs over, the one named last changes fastest.
Arguments:
- probes: float32 [8192, 256], P(('group', 'tile', 'list')), parts along dimension 0, may hold values from -6 to 6
- right_bases: bfloat16 [8, 1, 96, 1024], P(('group', 'tile'), None, 'list'), parts along dimension 0, may hold values from -0.1875 to 0.1875
- left_bases: bfloat16 [8, 1, 96, 1024], P(('group', 'tile'), None, 'list'), parts along dimension 0, may hold values from -0.625 to 0.625
- near_tiles: bfloat16 [8, 1024, 3, 1024], P(('group', 'tile'), None, None, 'list'), parts along dimension 0, may hold values from -0.109375 to 0.109375
- tile_ranks: int32 [8, 1], P(('group', 'tile')), parts along dimension 0, may hold values from 32 to 96
- column_rows: int32 [4, 1], P('tile'), may hold values from 0 to 3, as said below
- row_columns: int32 [4, 1], P('tile'), may hold values from 0 to 3, as said below
Outputs:
- product: float32 [8192, 256], P(('group', 'tile', 'list')), parts along dimension 0
The draws below stay inside these ranges and needn't reach their ends.
There are 2 independent parts, one for each index of `group`. The reference program is written for one: setup_inputs(seed, part) draws one part's arguments, and reference() takes and returns one part's arrays. A program takes and returns all parts, laid end to end along the dimension named above; an argument that names none is the same for every part. Nothing has to cross between parts.
Inputs may be any that keep to these rules, and one draw needn't show every extreme that they name: `column_rows`: each row j lists 1 distinct tile rows. Tile (i, j) is listed in row j here exactly when j is listed in row i of row_columns. A listed tile may lie beside the diagonal; its low-rank term then adds to the dense tile. `row_columns`: each row i lists 1 distinct tile columns, matching column_rows.
All inputs are finite; a program needn't handle non-finite values.
Results may differ from the reference program's by a relative error of at most 0.0048.
Values may be sent and summed in bfloat16 or wider, within the bound.
A program may use at most 64 MiB of HBM per device.

```python
import jax
import jax.numpy as jnp
from jax import lax

TILE = 1024
PROBES = 256
RMAX = 96
RMIN = 32
NT = 4
KT = 1
N = 4096


def pattern_parts(key):
    from_label = jax.random.permutation(jax.random.fold_in(key, 13), NT).astype(jnp.int32)
    to_label = from_label
    counting = jnp.arange(NT, dtype=jnp.int32)
    from_inverse = jnp.zeros((NT,), jnp.int32).at[from_label].set(counting)
    to_inverse = from_inverse
    magnitude = jnp.arange(KT, dtype=jnp.int32) + 1
    signs = jax.random.randint(jax.random.fold_in(key, 23), (KT,), 0, 2).astype(jnp.int32) * 2 - 1
    offsets = (magnitude * signs + NT) % NT
    order = jax.random.permutation(jax.random.fold_in(key, 19), KT).astype(jnp.int32)
    offsets = offsets[order]
    return (from_label, to_label, from_inverse, to_inverse, offsets)


def draw_column_rows(key, part):
    from_label, to_label, from_inverse, to_inverse, offsets = pattern_parts(key)
    return to_inverse[(from_label[:, None] + offsets[None, :]) % NT].astype(jnp.int32)


def draw_row_columns(key, part):
    from_label, to_label, from_inverse, to_inverse, offsets = pattern_parts(key)
    return from_inverse[(to_label[:, None] - offsets[None, :] + NT) % NT].astype(jnp.int32)


def draw_tile_ranks(key, part):
    entries = NT * KT
    values = jax.random.randint(jax.random.fold_in(key, 3), (entries,), RMIN, RMAX + 1)
    top_slot = jax.random.randint(jax.random.fold_in(key, 5), (), 0, entries)
    low_slot = (top_slot + 1 + jax.random.randint(jax.random.fold_in(key, 7), (), 0, entries - 1)) % entries
    values = values.at[top_slot].set(RMAX).at[low_slot].set(RMIN)
    return values.reshape(NT, KT).astype(jnp.int32)


def block_scale(key, dims, shards, smallest, high):
    gain, own = 1.0, jax.random.fold_in(key, 6)
    for axis_at, parts in shards:
        steps = jnp.exp(jax.random.uniform(jax.random.fold_in(own, axis_at), (parts,), jnp.float32, smallest / len(shards), high / len(shards)))
        gain = gain * jnp.repeat(steps, dims[axis_at] // parts).reshape([-1 if axis == axis_at else 1 for axis in range(len(dims))])
    return gain


def centred(stream_key, shape, spread, bound, split=(), kind=jnp.bfloat16):
    level = block_scale(stream_key, shape, split, -0.22, 0.18) if split else 1.0
    array = jax.random.normal(stream_key, shape, jnp.float32) * spread * level
    return jnp.minimum(jnp.maximum(array, -bound), bound).astype(kind)


def setup_inputs(seed: int = 0, part: int = 0) -> dict:
    arg_keys = jax.random.split(jax.random.key(seed), 8)
    part_keys = jax.random.split(jax.random.fold_in(arg_keys[7], part), 8)
    probes = centred(part_keys[0], (N, PROBES), 1.0, 6.0, ((0, 16),), jnp.float32)
    right_bases = centred(part_keys[1], (NT, KT, RMAX, TILE), TILE ** -0.5, 0.1875, ((0, 4), (2, 4)))
    left_bases = centred(part_keys[2], (NT, KT, RMAX, TILE), (KT * RMAX) ** -0.5, 0.625, ((0, 4), (2, 4)))
    near_tiles = centred(part_keys[3], (NT, TILE, 3, TILE), (3 * TILE) ** -0.5, 0.109375, ((0, 4), (3, 4)))
    tile_ranks = draw_tile_ranks(jax.random.fold_in(jax.random.fold_in(arg_keys[7], part), 71), part)
    column_rows = draw_column_rows(jax.random.fold_in(arg_keys[7], 71), part)
    row_columns = draw_row_columns(jax.random.fold_in(arg_keys[7], 71), part)
    return {"probes": probes, "right_bases": right_bases, "left_bases": left_bases, "near_tiles": near_tiles, "tile_ranks": tile_ranks, "column_rows": column_rows, "row_columns": row_columns}


def image_of(operand, right_bases, left_bases, near_tiles, tile_ranks, column_rows, row_columns):
    blocks = operand.reshape(NT, TILE, PROBES)
    rank_level = jnp.arange(RMAX, dtype=jnp.int32)

    def column_terms(col_index):
        flattened = right_bases[col_index].reshape(KT * RMAX, TILE)
        values = jnp.dot(flattened, blocks[col_index], preferred_element_type=jnp.float32)
        values = values.reshape(KT, RMAX, PROBES)
        rank_mask = rank_level[None, :] < tile_ranks[col_index][:, None]
        return jnp.where(rank_mask[:, :, None], values, 0.0).astype(jnp.bfloat16)

    coefficients = lax.map(column_terms, jnp.arange(NT, dtype=jnp.int32))
    empty = jnp.zeros((1, TILE, PROBES), operand.dtype)
    padded = jnp.concatenate([empty, blocks, empty], axis=0)

    def row_terms(row_index):
        sources = row_columns[row_index]
        matches = column_rows[sources] == row_index
        slot_index = jnp.argmax(matches, axis=1).astype(jnp.int32)
        selected = coefficients[sources, slot_index].reshape(KT * RMAX, PROBES)
        far_sum = jnp.dot(left_bases[row_index].reshape(KT * RMAX, TILE).T, selected, preferred_element_type=jnp.float32)
        window = lax.dynamic_slice_in_dim(padded, row_index, 3, 0).reshape(3 * TILE, PROBES)
        near_sum = jnp.dot(near_tiles[row_index].reshape(TILE, 3 * TILE), window, preferred_element_type=jnp.float32)
        return near_sum + far_sum

    rows_all = lax.map(row_terms, jnp.arange(NT, dtype=jnp.int32))
    return rows_all.reshape(N, PROBES)


def reference(probes, right_bases, left_bases, near_tiles, tile_ranks, column_rows, row_columns):
    probe_bf = probes.astype(jnp.bfloat16)
    first_pass = image_of(probe_bf, right_bases, left_bases, near_tiles, tile_ranks, column_rows, row_columns).astype(jnp.bfloat16)
    return image_of(first_pass, right_bases, left_bases, near_tiles, tile_ranks, column_rows, row_columns)
```

```python
import functools

import jax
import jax.numpy as jnp
from jax import lax
from jax.experimental import pallas as pl
from jax.experimental.pallas import tpu as pltpu
from jax.sharding import PartitionSpec as P

MESH = pl.DeviceIdType.MESH
BF16 = jnp.bfloat16
F32 = jnp.float32
CHUNKS = 2
FLIPS = ((0, 0), (0, 1), (1, 0), (1, 1))


def fused_kernel(
    tiles, near, right, left, probes, ranks, rows, out,
    near_v, probe_v, right_v, left_v, right_x, left_x, left_n, right_c, left_t, left_tn,
    row_send, row_recv, mix_part, mix_recv, mix,
    w, zbuf, stack, center, kept, osend, orecv, xsend, xrecv, fin,
    pc, prec, cbuf, crecv, sbuf, srecv, sbuf2, srecv2,
    local_sem, set_send, set_recv, side_send, side_recv, z_send, z_recv, p_send, p_recv,
    c_send, c_recv, s_send, s_recv, o_send, o_recv, x_send, x_recv,
):
    g, t, l = lax.axis_index("group"), lax.axis_index("tile"), lax.axis_index("list")
    x, c = l // 2, l % 2
    rank_part = right.shape[0]
    shard = probes.shape[0]
    width = probes.shape[1] // CHUNKS
    padding = right_c.shape[0] - 4 * rank_part

    def peer(k):
        return (x + FLIPS[k][0]) % 2 * 2 + (c + FLIPS[k][1]) % 2

    def joined(parts):
        rest = [jnp.zeros((padding, parts[0].shape[1]), F32)] if padding else []
        return jnp.concatenate([part.astype(F32) for part in parts] + rest, axis=0)

    loads = [pltpu.make_async_copy(probes, probe_v, local_sem.at[0])]
    for at, s in enumerate((1, 0, 2)):
        place = (2, 0, 1)[at]
        loads.append(
            pltpu.make_async_copy(
                near.at[s], near_v.at[:, :, pl.ds(place * shard, shard)], local_sem.at[1 + at]
            )
        )
    own = pl.ds(pl.multiple_of(l * shard, shard), shard)
    loads.insert(0, pltpu.make_async_copy(right, right_v, local_sem.at[4]))
    loads.insert(2, pltpu.make_async_copy(left, left_v, local_sem.at[5]))
    for load in loads:
        load.start()

    barrier = pltpu.get_barrier_semaphore()
    for k in (1, 2, 3):
        pl.semaphore_signal(barrier, inc=1, device_id=(g, t, peer(k)), device_id_type=MESH)
    for d in range(1, tiles):
        pl.semaphore_signal(barrier, inc=1, device_id=(g, (t + d) % tiles, l), device_id_type=MESH)

    for way, edge in ((0, 0), (1, tiles - 1)):

        @pl.when(t == edge)
        def _():
            zbuf[:, :, way * shard : (way + 1) * shard, :] = jnp.zeros((2, CHUNKS, shard, width), BF16)
            left_n[way] = jnp.zeros(left_n.shape[1:], BF16)
            row_recv[way] = jnp.full(row_recv.shape[1:], -1, jnp.int32)

    row_send[...] = jnp.full(row_send.shape, rows[0, 0], jnp.int32)

    loads[1].wait()
    for ch in range(CHUNKS):
        w[0, ch] = probe_v[:, ch * width : (ch + 1) * width].astype(BF16)
    pl.semaphore_wait(barrier, 3 + tiles - 1)

    sent = []

    def send(src, dst, ssem, rsem, tile, lst):
        copy = pltpu.make_async_remote_copy(
            src_ref=src, dst_ref=dst, send_sem=ssem, recv_sem=rsem,
            device_id=(g, tile, lst), device_id_type=MESH,
        )
        copy.start()
        sent.append(copy)
        return copy

    class Both:
        def __init__(self, src, dst, ssem, rsem):
            self.copies = [
                pltpu.make_async_remote_copy(
                    src_ref=src, dst_ref=dst(way), send_sem=ssem.at[way], recv_sem=rsem.at[way],
                    device_id=(g, (t + (1 if way == 0 else tiles - 1)) % tiles, l),
                    device_id_type=MESH,
                )
                for way in range(2)
            ]

        def each(self, act, holds):
            for copy, held in zip(self.copies, holds):

                @pl.when(held)
                def _(copy=copy):
                    act(copy)

        def start(self):
            self.each(lambda copy: copy.start(), (t < tiles - 1, t > 0))
            return self

        def wait_send(self):
            self.each(lambda copy: copy.wait_send(), (t < tiles - 1, t > 0))

        def wait_recv(self):
            self.each(lambda copy: copy.wait_recv(), (t > 0, t < tiles - 1))

    flying = {}

    def z_start(p, ch):
        flying["z", p, ch] = Both(
            w.at[p, ch], lambda way: zbuf.at[p, ch, pl.ds(way * shard, shard)],
            z_send.at[p, ch], z_recv.at[p, ch],
        ).start()
        sent.append(flying["z", p, ch])

    order = [((x + 1) % 2) * 2 + (1 - c), x * 2 + (1 - c), ((x + 1) % 2) * 2 + c, x * 2 + c]

    def stage_pc(p, ch):
        values = jnp.dot(right_c[...], w[p, ch], preferred_element_type=F32)
        for k in range(4):
            pc[p, ch, k] = values[k * rank_part : (k + 1) * rank_part].astype(BF16)
        for k in (1, 2, 3):
            flying["p", p, ch, k] = send(
                pc.at[p, ch, peer(k)], prec.at[p, ch, k - 1],
                p_send.at[p, ch, k - 1], p_recv.at[p, ch, k - 1], t, peer(k),
            )

    def stage_center(ch):
        for at in range(4):
            center[ch, at] = jnp.dot(
                near_v[order[at], :, 2 * shard : 3 * shard], w[0, ch], preferred_element_type=F32
            )

    def stage_b(p, ch, more=None):
        for k in (1, 2, 3):
            flying["p", p, ch, k].wait_recv()
        values = sum(prec[p, ch, k].astype(F32) for k in range(3)) + pc[p, ch, l].astype(F32)
        if more is not None:
            values = values + more
        level = l * rank_part + lax.broadcasted_iota(jnp.int32, values.shape, 0)
        cbuf[p, ch] = jnp.where(level < ranks[0, 0], values, 0.0).astype(BF16)
        for d in range(1, tiles):
            flying["c", p, ch, d] = send(
                cbuf.at[p, ch], crecv.at[p, ch, d - 1],
                c_send.at[p, ch, d - 1], c_recv.at[p, ch, d - 1], (t + d) % tiles, l,
            )

    def row_block(p, ch, at):
        if p == 0:
            return center[ch, at] + jnp.dot(
                near_v[order[at], :, 0 : 2 * shard], zbuf[0, ch], preferred_element_type=F32
            )
        return jnp.dot(near_v[order[at]], stack[ch], preferred_element_type=F32)

    def stage_c(p, ch):
        for at in range(4):
            value = row_block(p, ch, at)
            if at < 2:
                osend[p, ch, at] = value
                flying["o", p, ch, at] = send(
                    osend.at[p, ch, at], orecv.at[p, ch, at],
                    o_send.at[p, ch, at], o_recv.at[p, ch, at], t, peer(1),
                )
            else:
                kept[ch, at - 2] = value

    def stage_d(p, ch):
        flying["o", p, ch, 0].wait_recv()
        xsend[p, ch] = (kept[ch, 0] + orecv[p, ch, 0]).astype(BF16)
        flying["x", p, ch] = send(
            xsend.at[p, ch], xrecv.at[p, ch], x_send.at[p, ch], x_recv.at[p, ch], t, peer(2)
        )
        flying["o", p, ch, 1].wait_recv()
        fin[ch] = kept[ch, 1] + orecv[p, ch, 1]

    def stage_n(ch):
        flying["x", 0, ch].wait_recv()
        value = fin[ch] + xrecv[0, ch].astype(F32)
        fin[ch] = value
        w[1, ch] = value.astype(BF16)
        z_start(1, ch)
        stage_pc(1, ch)

    def stage_e(p, ch):
        blocks = [cbuf[p, ch].astype(F32)]
        for d in range(1, tiles):
            flying["c", p, ch, d].wait_recv()
            blocks.append(crecv[p, ch, d - 1].astype(F32))

        def chosen(wanted):
            value = jnp.zeros(blocks[0].shape, F32)
            for d in range(tiles):
                value = jnp.where(wanted == (t + tiles - d) % tiles, blocks[d], value)
            return value.astype(BF16)

        if p == 0:
            sbuf[ch, 0] = chosen(rows[0, 0])
            for way in range(2):
                sbuf[ch, 1 + way] = chosen(row_recv[way, 0:1, 0:width])
            source, held = sbuf.at[ch], srecv.at[ch, l]
        else:
            sbuf2[ch] = chosen(rows[0, 0])
            source, held = sbuf2.at[ch], srecv2.at[ch, l]
        for k in (1, 2, 3):
            flying["s", p, ch, k] = send(
                source, held, s_send.at[p, ch, k - 1], s_recv.at[p, ch, k - 1], t, peer(k),
            )
        if p == 0:
            srecv[ch, l] = sbuf[ch]
        else:
            srecv2[ch, l] = sbuf2[ch]

    def stage_g(ch):
        for k in (1, 2, 3):
            flying["s", 0, ch, k].wait_recv()
        of = [joined([srecv[ch, k, at] for k in range(4)]).astype(BF16) for at in range(3)]
        stage_b(1, ch, jnp.dot(mix[...], of[0], preferred_element_type=F32))
        far = jnp.dot(left_t[...], of[0], preferred_element_type=F32)
        stack[ch, 2 * shard : 3 * shard] = (fin[ch] + far).astype(BF16)
        flying["z", 1, ch].wait_recv()
        for way in range(2):
            far = jnp.dot(left_tn[way], of[1 + way], preferred_element_type=F32)
            part = slice(way * shard, (way + 1) * shard)
            stack[ch, part] = (zbuf[1, ch, part].astype(F32) + far).astype(BF16)

    def stage_f(ch):
        for k in (1, 2, 3):
            flying["s", 1, ch, k].wait_recv()
        coefficients = joined([srecv2[ch, k] for k in range(4)]).astype(BF16)
        far = fin[ch] + jnp.dot(left_t[...], coefficients, preferred_element_type=F32)
        flying["x", 1, ch].wait_recv()
        out[:, ch * width : (ch + 1) * width] = far + xrecv[1, ch].astype(F32)

    def bases(source, held, base):
        copies = []
        for k in (1, 2, 3):
            columns = pl.ds(pl.multiple_of(peer(k) * shard, shard), shard)
            copies.append(
                send(
                    source.at[:, columns], held.at[l],
                    set_send.at[base + k], set_recv.at[base + k], t, peer(k),
                )
            )
        held[l] = source[:, own]
        return copies

    loads[0].wait()
    right_copies = bases(right_v, right_x, 0)
    for ch in range(CHUNKS):
        z_start(0, ch)
    loads[2].wait()
    left_copies = bases(left_v, left_x, 4)
    row_copies = Both(row_send, lambda way: row_recv.at[way], side_send.at[0], side_recv.at[0]).start()
    sent.append(row_copies)
    loads[3].wait()
    for ch in range(CHUNKS):
        stage_center(ch)
    for copy in right_copies:
        copy.wait_recv()
    right_c[...] = joined([right_x[k] for k in range(4)]).astype(BF16)
    for ch in range(CHUNKS):
        stage_pc(0, ch)
    for copy in left_copies:
        copy.wait_recv()
    beside = Both(left_x, lambda way: left_n.at[way], side_send.at[1], side_recv.at[1]).start()
    sent.append(beside)
    left_t[...] = joined([left_x[k] for k in range(4)]).T.astype(BF16)
    loads[4].wait()
    loads[5].wait()
    for ch in range(CHUNKS):
        flying["z", 0, ch].wait_recv()
        stage_c(0, ch)
    stage_d(0, 0)
    for ch in range(CHUNKS):
        stage_b(0, ch)
    stage_d(0, 1)

    part = jnp.dot(right_c[...], left_t[...], preferred_element_type=F32)
    for k in range(4):
        mix_part[k] = part[k * rank_part : (k + 1) * rank_part]
    mix_copies = [
        send(mix_part.at[peer(k)], mix_recv.at[k - 1], set_send.at[8 + k], set_recv.at[8 + k], t, peer(k))
        for k in (1, 2, 3)
    ]
    beside.wait_recv()
    row_copies.wait_recv()
    for way in range(2):
        left_tn[way] = joined([left_n[way, k] for k in range(4)]).T.astype(BF16)

    stage_n(0)
    stage_e(0, 0)
    stage_n(1)
    stage_e(0, 1)
    for copy in mix_copies:
        copy.wait_recv()
    mix[...] = (mix_part[l] + mix_recv[0] + mix_recv[1] + mix_recv[2]).astype(BF16)
    stage_g(0)
    stage_c(1, 0)
    stage_g(1)
    stage_d(1, 0)
    stage_c(1, 1)
    stage_d(1, 1)
    stage_e(1, 0)
    stage_e(1, 1)
    for ch in range(CHUNKS):
        stage_f(ch)

    for copy in sent:
        copy.wait_send()


def fused(tiles, probes, right_bases, left_bases, near_tiles, tile_ranks, row_columns):
    rank_part = right_bases.shape[2]
    shard, probe_count = probes.shape
    width = probe_count // CHUNKS
    near = near_tiles[0].transpose(1, 0, 2).reshape(3, 4, shard, shard)
    both = (2, CHUNKS)
    full = -(-4 * rank_part // 128) * 128
    any_spec = pl.BlockSpec(memory_space=pltpu.HBM)
    smem_spec = pl.BlockSpec(memory_space=pltpu.SMEM)
    dma = pltpu.SemaphoreType.DMA
    return pl.pallas_call(
        functools.partial(fused_kernel, tiles),
        out_shape=jax.ShapeDtypeStruct((shard, probe_count), F32),
        in_specs=[any_spec] * 4 + [smem_spec] * 2,
        out_specs=pl.BlockSpec(memory_space=pltpu.VMEM),
        scratch_shapes=[
            pltpu.VMEM((4, shard, 3 * shard), BF16),
            pltpu.VMEM((shard, probe_count), F32),
            pltpu.VMEM((rank_part, 4 * shard), BF16),
            pltpu.VMEM((rank_part, 4 * shard), BF16),
            pltpu.VMEM((4, rank_part, shard), BF16),
            pltpu.VMEM((4, rank_part, shard), BF16),
            pltpu.VMEM((2, 4, rank_part, shard), BF16),
            pltpu.VMEM((full, shard), BF16),
            pltpu.VMEM((shard, full), BF16),
            pltpu.VMEM((2, shard, full), BF16),
            pltpu.VMEM((8, width), jnp.int32),
            pltpu.VMEM((2, 8, width), jnp.int32),
            pltpu.VMEM((4, rank_part, full), F32),
            pltpu.VMEM((3, rank_part, full), F32),
            pltpu.VMEM((rank_part, full), BF16),
            pltpu.VMEM(both + (shard, width), BF16),
            pltpu.VMEM(both + (2 * shard, width), BF16),
            pltpu.VMEM((CHUNKS, 3 * shard, width), BF16),
            pltpu.VMEM((CHUNKS, 4, shard, width), F32),
            pltpu.VMEM((CHUNKS, 2, shard, width), F32),
            pltpu.VMEM(both + (2, shard, width), F32),
            pltpu.VMEM(both + (2, shard, width), F32),
            pltpu.VMEM(both + (shard, width), BF16),
            pltpu.VMEM(both + (shard, width), BF16),
            pltpu.VMEM((CHUNKS, shard, width), F32),
            pltpu.VMEM(both + (4, rank_part, width), BF16),
            pltpu.VMEM(both + (3, rank_part, width), BF16),
            pltpu.VMEM(both + (rank_part, width), BF16),
            pltpu.VMEM(both + (tiles - 1, rank_part, width), BF16),
            pltpu.VMEM((CHUNKS, 3, rank_part, width), BF16),
            pltpu.VMEM((CHUNKS, 4, 3, rank_part, width), BF16),
            pltpu.VMEM((CHUNKS, rank_part, width), BF16),
            pltpu.VMEM((CHUNKS, 4, rank_part, width), BF16),
            dma((6,)), dma((12,)), dma((12,)), dma((2, 2)), dma((2, 2)), dma(both + (2,)), dma(both + (2,)),
            dma(both + (3,)), dma(both + (3,)), dma(both + (tiles - 1,)), dma(both + (tiles - 1,)),
            dma(both + (3,)), dma(both + (3,)), dma(both + (2,)), dma(both + (2,)),
            dma(both), dma(both),
        ],
        compiler_params=pltpu.CompilerParams(
            collective_id=0, has_side_effects=True, vmem_limit_bytes=67_043_328
        ),
    )(near, right_bases[0, 0], left_bases[0, 0], probes, tile_ranks, row_columns)


def shifted(block, axis, distance):
    devices = range(lax.axis_size(axis))
    route = [(i - distance, i) for i in devices if i - distance in devices]
    return lax.ppermute(block, axis, route)


def image_part(operand, right_bases, left_bases, near_tiles, tile_ranks, column_rows, row_columns):
    tile_slots = right_bases.shape[1]
    rank_part = right_bases.shape[2]
    tile_rows = right_bases.shape[3]
    probe_count = operand.shape[1]
    tile_count = lax.axis_size("tile")
    right_flat = right_bases.reshape(tile_slots * rank_part, tile_rows)
    left_flat = left_bases.reshape(tile_slots * rank_part, tile_rows)
    dense_flat = near_tiles.reshape(tile_rows, -1)
    values = jnp.dot(
        right_flat,
        lax.all_gather(operand, "list", axis=0, tiled=True),
        preferred_element_type=jnp.float32,
    )
    rank_level = lax.axis_index("list") * rank_part + lax.iota(jnp.int32, rank_part)
    rank_mask = rank_level[None, :] < tile_ranks[0][:, None]
    coefficients = jnp.where(
        rank_mask[:, :, None], values.reshape(tile_slots, rank_part, probe_count), 0.0
    ).astype(jnp.bfloat16)
    targets = (column_rows[0][None, :] == lax.iota(jnp.int32, tile_count)[:, None]).astype(
        jnp.bfloat16
    )
    outgoing = jnp.einsum(
        "dk,krp->drp", targets, coefficients, preferred_element_type=jnp.float32
    ).astype(jnp.bfloat16)
    sources = (row_columns[0][:, None] == lax.iota(jnp.int32, tile_count)[None, :]).astype(
        jnp.bfloat16
    )
    chosen = jnp.einsum(
        "kj,jrp->krp",
        sources,
        lax.all_to_all(outgoing, "tile", split_axis=0, concat_axis=0, tiled=True),
        preferred_element_type=jnp.float32,
    ).astype(jnp.bfloat16)
    chosen = chosen.reshape(tile_slots * rank_part, -1)
    far_sum = lax.dot_general(
        left_flat, chosen, (((0,), (0,)), ((), ())), preferred_element_type=jnp.float32
    )
    arrived = {}
    for offset in (1, -1):
        arrived[offset] = shifted(operand, "tile", offset)
    stacked = jnp.concatenate([arrived[1], operand, arrived[-1]], axis=0)
    near_sum = jnp.dot(dense_flat, stacked, preferred_element_type=jnp.float32)
    partial_image = near_sum + far_sum
    return lax.psum_scatter(partial_image, "list", scatter_dimension=0, tiled=True)


def local(probes, right_bases, left_bases, near_tiles, tile_ranks, column_rows, row_columns):
    list_count, tile_count = lax.axis_size("list"), lax.axis_size("tile")
    if list_count == 4 and right_bases.shape[1] == 1 and 2 < tile_count <= 8:
        return fused(
            tile_count, probes, right_bases, left_bases, near_tiles, tile_ranks, row_columns
        )
    probe_bf = probes.astype(jnp.bfloat16)
    first_pass = image_part(
        probe_bf, right_bases, left_bases, near_tiles, tile_ranks, column_rows, row_columns
    ).astype(jnp.bfloat16)
    return image_part(
        first_pass, right_bases, left_bases, near_tiles, tile_ranks, column_rows, row_columns
    )


def solution(mesh):
    placed = (
        P(("group", "tile", "list"), None),
        P(("group", "tile"), None, "list", None),
        P(("group", "tile"), None, "list", None),
        P(("group", "tile"), None, None, "list"),
        P(("group", "tile"), None),
        P("tile", None),
        P("tile", None),
    )
    return jax.shard_map(
        local,
        mesh=mesh,
        in_specs=placed,
        out_specs=P(("group", "tile", "list"), None),
        check_vma=False,
    )
```

```python
import functools

import jax
import jax.numpy as jnp
from jax import lax
from jax.experimental import pallas as pl
from jax.experimental.pallas import tpu as pltpu
from jax.sharding import PartitionSpec as P

MESH = pl.DeviceIdType.MESH
BF16 = jnp.bfloat16
F32 = jnp.float32
CHUNKS = 2
FLIPS = ((0, 0), (0, 1), (1, 0), (1, 1))


def fused_kernel(
    tiles, near, right, left, probes, ranks, rows, out,
    near_v, probe_v, right_v, left_v, right_x, left_x, left_n, right_c, left_t, left_tn,
    row_send, row_recv, mix_part, mix_recv, mix,
    w, zbuf, stack, center, kept, osend, orecv, xsend, xrecv, fin,
    pc, prec, cbuf, crecv, sbuf, srecv, sbuf2, srecv2,
    local_sem, set_send, set_recv, side_send, side_recv, z_send, z_recv, p_send, p_recv,
    c_send, c_recv, s_send, s_recv, o_send, o_recv, x_send, x_recv,
):
    g, t, l = lax.axis_index("group"), lax.axis_index("tile"), lax.axis_index("list")
    x, c = l // 2, l % 2
    rank_part = right.shape[0]
    shard = probes.shape[0]
    width = probes.shape[1] // CHUNKS
    padding = right_c.shape[0] - 4 * rank_part

    def peer(k):
        return (x + FLIPS[k][0]) % 2 * 2 + (c + FLIPS[k][1]) % 2

    def joined(parts):
        rest = [jnp.zeros((padding, parts[0].shape[1]), F32)] if padding else []
        return jnp.concatenate([part.astype(F32) for part in parts] + rest, axis=0)

    loads = [pltpu.make_async_copy(probes, probe_v, local_sem.at[0])]
    for at, s in enumerate((1, 0, 2)):
        place = (2, 0, 1)[at]
        loads.append(
            pltpu.make_async_copy(
                near.at[s], near_v.at[:, :, pl.ds(place * shard, shard)], local_sem.at[1 + at]
            )
        )
    own = pl.ds(pl.multiple_of(l * shard, shard), shard)
    loads.insert(0, pltpu.make_async_copy(right, right_v, local_sem.at[4]))
    loads.insert(2, pltpu.make_async_copy(left, left_v, local_sem.at[5]))
    for load in loads:
        load.start()

    barrier = pltpu.get_barrier_semaphore()
    for k in (1, 2, 3):
        pl.semaphore_signal(barrier, inc=1, device_id=(g, t, peer(k)), device_id_type=MESH)
    for d in range(1, tiles):
        pl.semaphore_signal(barrier, inc=1, device_id=(g, (t + d) % tiles, l), device_id_type=MESH)

    for way, edge in ((0, 0), (1, tiles - 1)):

        @pl.when(t == edge)
        def _():
            zbuf[:, :, way * shard : (way + 1) * shard, :] = jnp.zeros((2, CHUNKS, shard, width), BF16)
            left_n[way] = jnp.zeros(left_n.shape[1:], BF16)
            row_recv[way] = jnp.full(row_recv.shape[1:], -1, jnp.int32)

    row_send[...] = jnp.full(row_send.shape, rows[0, 0], jnp.int32)

    loads[1].wait()
    for ch in range(CHUNKS):
        w[0, ch] = probe_v[:, ch * width : (ch + 1) * width].astype(BF16)
    pl.semaphore_wait(barrier, 3 + tiles - 1)

    sent = []

    def send(src, dst, ssem, rsem, tile, lst):
        copy = pltpu.make_async_remote_copy(
            src_ref=src, dst_ref=dst, send_sem=ssem, recv_sem=rsem,
            device_id=(g, tile, lst), device_id_type=MESH,
        )
        copy.start()
        sent.append(copy)
        return copy

    class Both:
        def __init__(self, src, dst, ssem, rsem):
            self.copies = [
                pltpu.make_async_remote_copy(
                    src_ref=src, dst_ref=dst(way), send_sem=ssem.at[way], recv_sem=rsem.at[way],
                    device_id=(g, (t + (1 if way == 0 else tiles - 1)) % tiles, l),
                    device_id_type=MESH,
                )
                for way in range(2)
            ]

        def each(self, act, holds):
            for copy, held in zip(self.copies, holds):

                @pl.when(held)
                def _(copy=copy):
                    act(copy)

        def start(self):
            self.each(lambda copy: copy.start(), (t < tiles - 1, t > 0))
            return self

        def wait_send(self):
            self.each(lambda copy: copy.wait_send(), (t < tiles - 1, t > 0))

        def wait_recv(self):
            self.each(lambda copy: copy.wait_recv(), (t > 0, t < tiles - 1))

    flying = {}

    def z_start(p, ch):
        flying["z", p, ch] = Both(
            w.at[p, ch], lambda way: zbuf.at[p, ch, pl.ds(way * shard, shard)],
            z_send.at[p, ch], z_recv.at[p, ch],
        ).start()
        sent.append(flying["z", p, ch])

    order = [((x + 1) % 2) * 2 + (1 - c), x * 2 + (1 - c), ((x + 1) % 2) * 2 + c, x * 2 + c]

    def stage_pc(p, ch):
        values = jnp.dot(right_c[...], w[p, ch], preferred_element_type=F32)
        for k in range(4):
            pc[p, ch, k] = values[k * rank_part : (k + 1) * rank_part].astype(BF16)
        for k in (1, 2, 3):
            flying["p", p, ch, k] = send(
                pc.at[p, ch, peer(k)], prec.at[p, ch, k - 1],
                p_send.at[p, ch, k - 1], p_recv.at[p, ch, k - 1], t, peer(k),
            )

    def stage_center(ch):
        for at in range(4):
            center[ch, at] = jnp.dot(
                near_v[order[at], :, 2 * shard : 3 * shard], w[0, ch], preferred_element_type=F32
            )

    def stage_b(p, ch, more=None):
        for k in (1, 2, 3):
            flying["p", p, ch, k].wait_recv()
        values = sum(prec[p, ch, k].astype(F32) for k in range(3)) + pc[p, ch, l].astype(F32)
        if more is not None:
            values = values + more
        level = l * rank_part + lax.broadcasted_iota(jnp.int32, values.shape, 0)
        cbuf[p, ch] = jnp.where(level < ranks[0, 0], values, 0.0).astype(BF16)
        for d in range(1, tiles):
            flying["c", p, ch, d] = send(
                cbuf.at[p, ch], crecv.at[p, ch, d - 1],
                c_send.at[p, ch, d - 1], c_recv.at[p, ch, d - 1], (t + d) % tiles, l,
            )

    def row_block(p, ch, at):
        if p == 0:
            return center[ch, at] + jnp.dot(
                near_v[order[at], :, 0 : 2 * shard], zbuf[0, ch], preferred_element_type=F32
            )
        return jnp.dot(near_v[order[at]], stack[ch], preferred_element_type=F32)

    def stage_c(p, ch):
        for at in range(4):
            value = row_block(p, ch, at)
            if at < 2:
                osend[p, ch, at] = value
                flying["o", p, ch, at] = send(
                    osend.at[p, ch, at], orecv.at[p, ch, at],
                    o_send.at[p, ch, at], o_recv.at[p, ch, at], t, peer(1),
                )
            else:
                kept[ch, at - 2] = value

    def stage_d(p, ch):
        flying["o", p, ch, 0].wait_recv()
        xsend[p, ch] = (kept[ch, 0] + orecv[p, ch, 0]).astype(BF16)
        flying["x", p, ch] = send(
            xsend.at[p, ch], xrecv.at[p, ch], x_send.at[p, ch], x_recv.at[p, ch], t, peer(2)
        )
        flying["o", p, ch, 1].wait_recv()
        fin[ch] = kept[ch, 1] + orecv[p, ch, 1]

    def stage_n(ch):
        flying["x", 0, ch].wait_recv()
        value = fin[ch] + xrecv[0, ch].astype(F32)
        fin[ch] = value
        w[1, ch] = value.astype(BF16)
        z_start(1, ch)
        stage_pc(1, ch)

    def stage_e(p, ch):
        blocks = [cbuf[p, ch].astype(F32)]
        for d in range(1, tiles):
            flying["c", p, ch, d].wait_recv()
            blocks.append(crecv[p, ch, d - 1].astype(F32))

        def chosen(wanted):
            value = jnp.zeros(blocks[0].shape, F32)
            for d in range(tiles):
                value = jnp.where(wanted == (t + tiles - d) % tiles, blocks[d], value)
            return value.astype(BF16)

        if p == 0:
            sbuf[ch, 0] = chosen(rows[0, 0])
            for way in range(2):
                sbuf[ch, 1 + way] = chosen(row_recv[way, 0:1, 0:width])
            source, held = sbuf.at[ch], srecv.at[ch, l]
        else:
            sbuf2[ch] = chosen(rows[0, 0])
            source, held = sbuf2.at[ch], srecv2.at[ch, l]
        for k in (1, 2, 3):
            flying["s", p, ch, k] = send(
                source, held, s_send.at[p, ch, k - 1], s_recv.at[p, ch, k - 1], t, peer(k),
            )
        if p == 0:
            srecv[ch, l] = sbuf[ch]
        else:
            srecv2[ch, l] = sbuf2[ch]

    def stage_g(ch):
        for k in (1, 2, 3):
            flying["s", 0, ch, k].wait_recv()
        of = [joined([srecv[ch, k, at] for k in range(4)]).astype(BF16) for at in range(3)]
        stage_b(1, ch, jnp.dot(mix[...], of[0], preferred_element_type=F32))
        far = jnp.dot(left_t[...], of[0], preferred_element_type=F32)
        stack[ch, 2 * shard : 3 * shard] = (fin[ch] + far).astype(BF16)
        flying["z", 1, ch].wait_recv()
        for way in range(2):
            far = jnp.dot(left_tn[way], of[1 + way], preferred_element_type=F32)
            part = slice(way * shard, (way + 1) * shard)
            stack[ch, part] = (zbuf[1, ch, part].astype(F32) + far).astype(BF16)

    def stage_f(ch):
        for k in (1, 2, 3):
            flying["s", 1, ch, k].wait_recv()
        coefficients = joined([srecv2[ch, k] for k in range(4)]).astype(BF16)
        far = fin[ch] + jnp.dot(left_t[...], coefficients, preferred_element_type=F32)
        flying["x", 1, ch].wait_recv()
        out[:, ch * width : (ch + 1) * width] = far + xrecv[1, ch].astype(F32)

    def bases(source, held, base):
        copies = []
        for k in (1, 2, 3):
            columns = pl.ds(pl.multiple_of(peer(k) * shard, shard), shard)
            copies.append(
                send(
                    source.at[:, columns], held.at[l],
                    set_send.at[base + k], set_recv.at[base + k], t, peer(k),
                )
            )
        held[l] = source[:, own]
        return copies

    loads[0].wait()
    right_copies = bases(right_v, right_x, 0)
    for ch in range(CHUNKS):
        z_start(0, ch)
    loads[2].wait()
    left_copies = bases(left_v, left_x, 4)
    row_copies = Both(row_send, lambda way: row_recv.at[way], side_send.at[0], side_recv.at[0]).start()
    sent.append(row_copies)
    loads[3].wait()
    for ch in range(CHUNKS):
        stage_center(ch)
    for copy in right_copies:
        copy.wait_recv()
    right_c[...] = joined([right_x[k] for k in range(4)]).astype(BF16)
    for ch in range(CHUNKS):
        stage_pc(0, ch)
    for copy in left_copies:
        copy.wait_recv()
    beside = Both(left_x, lambda way: left_n.at[way], side_send.at[1], side_recv.at[1]).start()
    sent.append(beside)
    left_t[...] = joined([left_x[k] for k in range(4)]).T.astype(BF16)
    loads[4].wait()
    loads[5].wait()
    for ch in range(CHUNKS):
        flying["z", 0, ch].wait_recv()
        stage_c(0, ch)
    stage_d(0, 0)
    for ch in range(CHUNKS):
        stage_b(0, ch)
    stage_d(0, 1)

    part = jnp.dot(right_c[...], left_t[...], preferred_element_type=F32)
    for k in range(4):
        mix_part[k] = part[k * rank_part : (k + 1) * rank_part]
    mix_copies = [
        send(mix_part.at[peer(k)], mix_recv.at[k - 1], set_send.at[8 + k], set_recv.at[8 + k], t, peer(k))
        for k in (1, 2, 3)
    ]
    beside.wait_recv()
    row_copies.wait_recv()
    for way in range(2):
        left_tn[way] = joined([left_n[way, k] for k in range(4)]).T.astype(BF16)

    stage_n(0)
    stage_e(0, 0)
    stage_n(1)
    stage_e(0, 1)
    for copy in mix_copies:
        copy.wait_recv()
    mix[...] = (mix_part[l] + mix_recv[0] + mix_recv[1] + mix_recv[2]).astype(BF16)
    stage_g(0)
    stage_c(1, 0)
    stage_g(1)
    stage_d(1, 0)
    stage_c(1, 1)
    stage_d(1, 1)
    stage_e(1, 0)
    stage_e(1, 1)
    for ch in range(CHUNKS):
        stage_f(ch)

    for copy in sent:
        copy.wait_send()


def fused(tiles, probes, right_bases, left_bases, near_tiles, tile_ranks, row_columns):
    rank_part = right_bases.shape[2]
    shard, probe_count = probes.shape
    width = probe_count // CHUNKS
    near = near_tiles[0].transpose(1, 0, 2).reshape(3, 4, shard, shard)
    both = (2, CHUNKS)
    full = -(-4 * rank_part // 128) * 128
    any_spec = pl.BlockSpec(memory_space=pltpu.HBM)
    smem_spec = pl.BlockSpec(memory_space=pltpu.SMEM)
    dma = pltpu.SemaphoreType.DMA
    return pl.pallas_call(
        functools.partial(fused_kernel, tiles),
        out_shape=pltpu.VMEM((shard, probe_count), F32),
        in_specs=[any_spec] * 4 + [smem_spec] * 2,
        out_specs=pl.BlockSpec(memory_space=pltpu.VMEM),
        scratch_shapes=[
            pltpu.VMEM((4, shard, 3 * shard), BF16),
            pltpu.VMEM((shard, probe_count), F32),
            pltpu.VMEM((rank_part, 4 * shard), BF16),
            pltpu.VMEM((rank_part, 4 * shard), BF16),
            pltpu.VMEM((4, rank_part, shard), BF16),
            pltpu.VMEM((4, rank_part, shard), BF16),
            pltpu.VMEM((2, 4, rank_part, shard), BF16),
            pltpu.VMEM((full, shard), BF16),
            pltpu.VMEM((shard, full), BF16),
            pltpu.VMEM((2, shard, full), BF16),
            pltpu.VMEM((8, width), jnp.int32),
            pltpu.VMEM((2, 8, width), jnp.int32),
            pltpu.VMEM((4, rank_part, full), F32),
            pltpu.VMEM((3, rank_part, full), F32),
            pltpu.VMEM((rank_part, full), BF16),
            pltpu.VMEM(both + (shard, width), BF16),
            pltpu.VMEM(both + (2 * shard, width), BF16),
            pltpu.VMEM((CHUNKS, 3 * shard, width), BF16),
            pltpu.VMEM((CHUNKS, 4, shard, width), F32),
            pltpu.VMEM((CHUNKS, 2, shard, width), F32),
            pltpu.VMEM(both + (2, shard, width), F32),
            pltpu.VMEM(both + (2, shard, width), F32),
            pltpu.VMEM(both + (shard, width), BF16),
            pltpu.VMEM(both + (shard, width), BF16),
            pltpu.VMEM((CHUNKS, shard, width), F32),
            pltpu.VMEM(both + (4, rank_part, width), BF16),
            pltpu.VMEM(both + (3, rank_part, width), BF16),
            pltpu.VMEM(both + (rank_part, width), BF16),
            pltpu.VMEM(both + (tiles - 1, rank_part, width), BF16),
            pltpu.VMEM((CHUNKS, 3, rank_part, width), BF16),
            pltpu.VMEM((CHUNKS, 4, 3, rank_part, width), BF16),
            pltpu.VMEM((CHUNKS, rank_part, width), BF16),
            pltpu.VMEM((CHUNKS, 4, rank_part, width), BF16),
            dma((6,)), dma((12,)), dma((12,)), dma((2, 2)), dma((2, 2)), dma(both + (2,)), dma(both + (2,)),
            dma(both + (3,)), dma(both + (3,)), dma(both + (tiles - 1,)), dma(both + (tiles - 1,)),
            dma(both + (3,)), dma(both + (3,)), dma(both + (2,)), dma(both + (2,)),
            dma(both), dma(both),
        ],
        compiler_params=pltpu.CompilerParams(
            collective_id=0, has_side_effects=True, vmem_limit_bytes=67_043_328 - 8 * shard * probe_count
        ),
    )(near, right_bases[0, 0], left_bases[0, 0], probes, tile_ranks, row_columns)


def shifted(block, axis, distance):
    devices = range(lax.axis_size(axis))
    route = [(i - distance, i) for i in devices if i - distance in devices]
    return lax.ppermute(block, axis, route)


def image_part(operand, right_bases, left_bases, near_tiles, tile_ranks, column_rows, row_columns):
    tile_slots = right_bases.shape[1]
    rank_part = right_bases.shape[2]
    tile_rows = right_bases.shape[3]
    probe_count = operand.shape[1]
    tile_count = lax.axis_size("tile")
    right_flat = right_bases.reshape(tile_slots * rank_part, tile_rows)
    left_flat = left_bases.reshape(tile_slots * rank_part, tile_rows)
    dense_flat = near_tiles.reshape(tile_rows, -1)
    values = jnp.dot(
        right_flat,
        lax.all_gather(operand, "list", axis=0, tiled=True),
        preferred_element_type=jnp.float32,
    )
    rank_level = lax.axis_index("list") * rank_part + lax.iota(jnp.int32, rank_part)
    rank_mask = rank_level[None, :] < tile_ranks[0][:, None]
    coefficients = jnp.where(
        rank_mask[:, :, None], values.reshape(tile_slots, rank_part, probe_count), 0.0
    ).astype(jnp.bfloat16)
    targets = (column_rows[0][None, :] == lax.iota(jnp.int32, tile_count)[:, None]).astype(
        jnp.bfloat16
    )
    outgoing = jnp.einsum(
        "dk,krp->drp", targets, coefficients, preferred_element_type=jnp.float32
    ).astype(jnp.bfloat16)
    sources = (row_columns[0][:, None] == lax.iota(jnp.int32, tile_count)[None, :]).astype(
        jnp.bfloat16
    )
    chosen = jnp.einsum(
        "kj,jrp->krp",
        sources,
        lax.all_to_all(outgoing, "tile", split_axis=0, concat_axis=0, tiled=True),
        preferred_element_type=jnp.float32,
    ).astype(jnp.bfloat16)
    chosen = chosen.reshape(tile_slots * rank_part, -1)
    far_sum = lax.dot_general(
        left_flat, chosen, (((0,), (0,)), ((), ())), preferred_element_type=jnp.float32
    )
    arrived = {}
    for offset in (1, -1):
        arrived[offset] = shifted(operand, "tile", offset)
    stacked = jnp.concatenate([arrived[1], operand, arrived[-1]], axis=0)
    near_sum = jnp.dot(dense_flat, stacked, preferred_element_type=jnp.float32)
    partial_image = near_sum + far_sum
    return lax.psum_scatter(partial_image, "list", scatter_dimension=0, tiled=True)


def local(probes, right_bases, left_bases, near_tiles, tile_ranks, column_rows, row_columns):
    list_count, tile_count = lax.axis_size("list"), lax.axis_size("tile")
    if list_count == 4 and right_bases.shape[1] == 1 and 2 < tile_count <= 8:
        return fused(
            tile_count, probes, right_bases, left_bases, near_tiles, tile_ranks, row_columns
        )
    probe_bf = probes.astype(jnp.bfloat16)
    first_pass = image_part(
        probe_bf, right_bases, left_bases, near_tiles, tile_ranks, column_rows, row_columns
    ).astype(jnp.bfloat16)
    return image_part(
        first_pass, right_bases, left_bases, near_tiles, tile_ranks, column_rows, row_columns
    )


def solution(mesh):
    placed = (
        P(("group", "tile", "list"), None),
        P(("group", "tile"), None, "list", None),
        P(("group", "tile"), None, "list", None),
        P(("group", "tile"), None, None, "list"),
        P(("group", "tile"), None),
        P("tile", None),
        P("tile", None),
    )
    return jax.shard_map(
        local,
        mesh=mesh,
        in_specs=placed,
        out_specs=P(("group", "tile", "list"), None),
        check_vma=False,
    )
```

```python
import functools

import jax
import jax.numpy as jnp
from jax import lax
from jax.experimental import pallas as pl
from jax.experimental.pallas import tpu as pltpu
from jax.sharding import PartitionSpec as P

MESH = pl.DeviceIdType.MESH
BF16 = jnp.bfloat16
F32 = jnp.float32
CHUNKS = 2
FLIPS = ((0, 0), (0, 1), (1, 0), (1, 1))


def fused_kernel(
    tiles, near, right, left, probes, ranks, rows, out,
    near_v, probe_v, right_v, left_v, right_x, left_x, left_n, right_c, left_t, left_tn,
    row_send, row_recv, mix_part, mix_recv, mix,
    w, zbuf, stack, center, kept, osend, orecv, xsend, xrecv, fin,
    pc, prec, cbuf, crecv, sbuf, srecv, sbuf2, srecv2,
    local_sem, send_sem, set_recv, side_recv, z_recv, p_recv, c_recv, s_recv, o_recv, x_recv,
):
    g, t, l = lax.axis_index("group"), lax.axis_index("tile"), lax.axis_index("list")
    x, c = l // 2, l % 2
    rank_part = right.shape[0]
    shard = probes.shape[0]
    width = probes.shape[1] // CHUNKS
    padding = right_c.shape[0] - 4 * rank_part

    def peer(k):
        return (x + FLIPS[k][0]) % 2 * 2 + (c + FLIPS[k][1]) % 2

    def joined(parts):
        rest = [jnp.zeros((padding, parts[0].shape[1]), F32)] if padding else []
        return jnp.concatenate([part.astype(F32) for part in parts] + rest, axis=0)

    loads = [pltpu.make_async_copy(probes, probe_v, local_sem.at[0])]
    for at, s in enumerate((1, 0, 2)):
        place = (2, 0, 1)[at]
        loads.append(
            pltpu.make_async_copy(
                near.at[s], near_v.at[:, :, pl.ds(place * shard, shard)], local_sem.at[1 + at]
            )
        )
    own = pl.ds(pl.multiple_of(l * shard, shard), shard)
    loads.insert(0, pltpu.make_async_copy(right, right_v, local_sem.at[4]))
    loads.insert(2, pltpu.make_async_copy(left, left_v, local_sem.at[5]))
    for load in loads:
        load.start()

    barrier = pltpu.get_barrier_semaphore()
    for k in (1, 2, 3):
        pl.semaphore_signal(barrier, inc=1, device_id=(g, t, peer(k)), device_id_type=MESH)
    for d in range(1, tiles):
        pl.semaphore_signal(barrier, inc=1, device_id=(g, (t + d) % tiles, l), device_id_type=MESH)

    for way, edge in ((0, 0), (1, tiles - 1)):

        @pl.when(t == edge)
        def _():
            zbuf[:, :, way * shard : (way + 1) * shard, :] = jnp.zeros((2, CHUNKS, shard, width), BF16)
            left_n[way] = jnp.zeros(left_n.shape[1:], BF16)
            row_recv[way] = jnp.full(row_recv.shape[1:], -1, jnp.int32)

    row_send[...] = jnp.full(row_send.shape, rows[0, 0], jnp.int32)

    loads[1].wait()
    for ch in range(CHUNKS):
        w[0, ch] = probe_v[:, ch * width : (ch + 1) * width].astype(BF16)
    pl.semaphore_wait(barrier, 3 + tiles - 1)

    sent = []

    def arrive(held, sem):
        pltpu.make_async_copy(held, held, sem).wait()

    def send(src, dst, rsem, tile, lst):
        copy = pltpu.make_async_remote_copy(
            src_ref=src, dst_ref=dst, send_sem=send_sem, recv_sem=rsem,
            device_id=(g, tile, lst), device_id_type=MESH,
        )
        copy.start()
        sent.append(copy)
        return copy

    class Both:
        def __init__(self, src, dst, rsem):
            self.copies = [
                pltpu.make_async_remote_copy(
                    src_ref=src, dst_ref=dst(way), send_sem=send_sem, recv_sem=rsem.at[way],
                    device_id=(g, (t + (1 if way == 0 else tiles - 1)) % tiles, l),
                    device_id_type=MESH,
                )
                for way in range(2)
            ]

        def each(self, act, holds):
            for copy, held in zip(self.copies, holds):

                @pl.when(held)
                def _(copy=copy):
                    act(copy)

        def start(self):
            self.each(lambda copy: copy.start(), (t < tiles - 1, t > 0))
            return self

        def wait_send(self):
            self.each(lambda copy: copy.wait_send(), (t < tiles - 1, t > 0))

        def wait_recv(self):
            self.each(lambda copy: copy.wait_recv(), (t > 0, t < tiles - 1))

    flying = {}

    def z_start(p, ch):
        flying["z", p, ch] = Both(
            w.at[p, ch], lambda way: zbuf.at[p, ch, pl.ds(way * shard, shard)],
            z_recv.at[p, ch],
        ).start()
        sent.append(flying["z", p, ch])

    order = [((x + 1) % 2) * 2 + (1 - c), x * 2 + (1 - c), ((x + 1) % 2) * 2 + c, x * 2 + c]

    def stage_pc(p, ch):
        values = jnp.dot(right_c[...], w[p, ch], preferred_element_type=F32)
        for k in range(4):
            pc[p, ch, k] = values[k * rank_part : (k + 1) * rank_part].astype(BF16)
        for k in (1, 2, 3):
            send(pc.at[p, ch, peer(k)], prec.at[p, ch, k - 1], p_recv.at[p, ch], t, peer(k))

    def stage_center(ch):
        for at in range(4):
            center[ch, at] = jnp.dot(
                near_v[order[at], :, 2 * shard : 3 * shard], w[0, ch], preferred_element_type=F32
            )

    def stage_b(p, ch, more=None):
        arrive(prec.at[p, ch], p_recv.at[p, ch])
        values = sum(prec[p, ch, k].astype(F32) for k in range(3)) + pc[p, ch, l].astype(F32)
        if more is not None:
            values = values + more
        level = l * rank_part + lax.broadcasted_iota(jnp.int32, values.shape, 0)
        cbuf[p, ch] = jnp.where(level < ranks[0, 0], values, 0.0).astype(BF16)
        for d in range(1, tiles):
            send(cbuf.at[p, ch], crecv.at[p, ch, d - 1], c_recv.at[p, ch], (t + d) % tiles, l)

    def row_block(p, ch, at):
        if p == 0:
            return center[ch, at] + jnp.dot(
                near_v[order[at], :, 0 : 2 * shard], zbuf[0, ch], preferred_element_type=F32
            )
        return jnp.dot(near_v[order[at]], stack[ch], preferred_element_type=F32)

    def stage_c(p, ch):
        for at in range(4):
            value = row_block(p, ch, at)
            if at < 2:
                osend[p, ch, at] = value
                flying["o", p, ch, at] = send(
                    osend.at[p, ch, at], orecv.at[p, ch, at], o_recv.at[p, ch, at], t, peer(1)
                )
            else:
                kept[ch, at - 2] = value

    def stage_d(p, ch):
        flying["o", p, ch, 0].wait_recv()
        xsend[p, ch] = (kept[ch, 0] + orecv[p, ch, 0]).astype(BF16)
        flying["x", p, ch] = send(
            xsend.at[p, ch], xrecv.at[p, ch], x_recv.at[p, ch], t, peer(2)
        )
        flying["o", p, ch, 1].wait_recv()
        fin[ch] = kept[ch, 1] + orecv[p, ch, 1]

    def stage_n(ch):
        flying["x", 0, ch].wait_recv()
        value = fin[ch] + xrecv[0, ch].astype(F32)
        fin[ch] = value
        w[1, ch] = value.astype(BF16)
        z_start(1, ch)
        stage_pc(1, ch)

    def stage_e(p, ch):
        arrive(crecv.at[p, ch], c_recv.at[p, ch])
        blocks = [cbuf[p, ch].astype(F32)]
        for d in range(1, tiles):
            blocks.append(crecv[p, ch, d - 1].astype(F32))

        def chosen(wanted):
            value = jnp.zeros(blocks[0].shape, F32)
            for d in range(tiles):
                value = jnp.where(wanted == (t + tiles - d) % tiles, blocks[d], value)
            return value.astype(BF16)

        if p == 0:
            sbuf[ch, 0] = chosen(rows[0, 0])
            for way in range(2):
                sbuf[ch, 1 + way] = chosen(row_recv[way, 0:1, 0:width])
            source, held = sbuf.at[ch], srecv.at[ch, l]
        else:
            sbuf2[ch] = chosen(rows[0, 0])
            source, held = sbuf2.at[ch], srecv2.at[ch, l]
        for k in (1, 2, 3):
            send(source, held, s_recv.at[p, ch], t, peer(k))
        if p == 0:
            srecv[ch, l] = sbuf[ch]
        else:
            srecv2[ch, l] = sbuf2[ch]

    def stage_g(ch):
        arrive(srecv.at[ch, pl.ds(0, 3)], s_recv.at[0, ch])
        of = [joined([srecv[ch, k, at] for k in range(4)]).astype(BF16) for at in range(3)]
        stage_b(1, ch, jnp.dot(mix[...], of[0], preferred_element_type=F32))
        far = jnp.dot(left_t[...], of[0], preferred_element_type=F32)
        stack[ch, 2 * shard : 3 * shard] = (fin[ch] + far).astype(BF16)
        flying["z", 1, ch].wait_recv()
        for way in range(2):
            far = jnp.dot(left_tn[way], of[1 + way], preferred_element_type=F32)
            part = slice(way * shard, (way + 1) * shard)
            stack[ch, part] = (zbuf[1, ch, part].astype(F32) + far).astype(BF16)

    def stage_f(ch):
        arrive(srecv2.at[ch, pl.ds(0, 3)], s_recv.at[1, ch])
        coefficients = joined([srecv2[ch, k] for k in range(4)]).astype(BF16)
        far = fin[ch] + jnp.dot(left_t[...], coefficients, preferred_element_type=F32)
        flying["x", 1, ch].wait_recv()
        out[:, ch * width : (ch + 1) * width] = far + xrecv[1, ch].astype(F32)

    def bases(source, held, at):
        for k in (1, 2, 3):
            columns = pl.ds(pl.multiple_of(peer(k) * shard, shard), shard)
            send(source.at[:, columns], held.at[l], set_recv.at[at], t, peer(k))
        held[l] = source[:, own]

    loads[0].wait()
    bases(right_v, right_x, 0)
    for ch in range(CHUNKS):
        z_start(0, ch)
    loads[2].wait()
    bases(left_v, left_x, 1)
    row_copies = Both(row_send, lambda way: row_recv.at[way], side_recv.at[0]).start()
    sent.append(row_copies)
    loads[3].wait()
    for ch in range(CHUNKS):
        stage_center(ch)
    arrive(right_x.at[pl.ds(0, 3)], set_recv.at[0])
    right_c[...] = joined([right_x[k] for k in range(4)]).astype(BF16)
    for ch in range(CHUNKS):
        stage_pc(0, ch)
    arrive(left_x.at[pl.ds(0, 3)], set_recv.at[1])
    beside = Both(left_x, lambda way: left_n.at[way], side_recv.at[1]).start()
    sent.append(beside)
    left_t[...] = joined([left_x[k] for k in range(4)]).T.astype(BF16)
    loads[4].wait()
    loads[5].wait()
    for ch in range(CHUNKS):
        flying["z", 0, ch].wait_recv()
        stage_c(0, ch)
    stage_d(0, 0)
    for ch in range(CHUNKS):
        stage_b(0, ch)
    stage_d(0, 1)

    part = jnp.dot(right_c[...], left_t[...], preferred_element_type=F32)
    for k in range(4):
        mix_part[k] = part[k * rank_part : (k + 1) * rank_part]
    for k in (1, 2, 3):
        send(mix_part.at[peer(k)], mix_recv.at[k - 1], set_recv.at[2], t, peer(k))
    beside.wait_recv()
    row_copies.wait_recv()
    for way in range(2):
        left_tn[way] = joined([left_n[way, k] for k in range(4)]).T.astype(BF16)

    stage_n(0)
    stage_e(0, 0)
    stage_n(1)
    stage_e(0, 1)
    arrive(mix_recv, set_recv.at[2])
    mix[...] = (mix_part[l] + mix_recv[0] + mix_recv[1] + mix_recv[2]).astype(BF16)
    stage_g(0)
    stage_c(1, 0)
    stage_g(1)
    stage_d(1, 0)
    stage_c(1, 1)
    stage_e(1, 0)
    stage_d(1, 1)
    stage_e(1, 1)
    for ch in range(CHUNKS):
        stage_f(ch)

    for copy in sent:
        copy.wait_send()


def fused(tiles, probes, right_bases, left_bases, near_tiles, tile_ranks, row_columns):
    rank_part = right_bases.shape[2]
    shard, probe_count = probes.shape
    width = probe_count // CHUNKS
    near = near_tiles[0].transpose(1, 0, 2).reshape(3, 4, shard, shard)
    both = (2, CHUNKS)
    full = -(-4 * rank_part // 128) * 128
    any_spec = pl.BlockSpec(memory_space=pltpu.HBM)
    smem_spec = pl.BlockSpec(memory_space=pltpu.SMEM)
    dma = pltpu.SemaphoreType.DMA
    return pl.pallas_call(
        functools.partial(fused_kernel, tiles),
        out_shape=pltpu.VMEM((shard, probe_count), F32),
        in_specs=[any_spec] * 4 + [smem_spec] * 2,
        out_specs=pl.BlockSpec(memory_space=pltpu.VMEM),
        scratch_shapes=[
            pltpu.VMEM((4, shard, 3 * shard), BF16),
            pltpu.VMEM((shard, probe_count), F32),
            pltpu.VMEM((rank_part, 4 * shard), BF16),
            pltpu.VMEM((rank_part, 4 * shard), BF16),
            pltpu.VMEM((4, rank_part, shard), BF16),
            pltpu.VMEM((4, rank_part, shard), BF16),
            pltpu.VMEM((2, 4, rank_part, shard), BF16),
            pltpu.VMEM((full, shard), BF16),
            pltpu.VMEM((shard, full), BF16),
            pltpu.VMEM((2, shard, full), BF16),
            pltpu.VMEM((8, width), jnp.int32),
            pltpu.VMEM((2, 8, width), jnp.int32),
            pltpu.VMEM((4, rank_part, full), F32),
            pltpu.VMEM((3, rank_part, full), F32),
            pltpu.VMEM((rank_part, full), BF16),
            pltpu.VMEM(both + (shard, width), BF16),
            pltpu.VMEM(both + (2 * shard, width), BF16),
            pltpu.VMEM((CHUNKS, 3 * shard, width), BF16),
            pltpu.VMEM((CHUNKS, 4, shard, width), F32),
            pltpu.VMEM((CHUNKS, 2, shard, width), F32),
            pltpu.VMEM(both + (2, shard, width), F32),
            pltpu.VMEM(both + (2, shard, width), F32),
            pltpu.VMEM(both + (shard, width), BF16),
            pltpu.VMEM(both + (shard, width), BF16),
            pltpu.VMEM((CHUNKS, shard, width), F32),
            pltpu.VMEM(both + (4, rank_part, width), BF16),
            pltpu.VMEM(both + (3, rank_part, width), BF16),
            pltpu.VMEM(both + (rank_part, width), BF16),
            pltpu.VMEM(both + (tiles - 1, rank_part, width), BF16),
            pltpu.VMEM((CHUNKS, 3, rank_part, width), BF16),
            pltpu.VMEM((CHUNKS, 4, 3, rank_part, width), BF16),
            pltpu.VMEM((CHUNKS, rank_part, width), BF16),
            pltpu.VMEM((CHUNKS, 4, rank_part, width), BF16),
            dma((6,)), dma, dma((3,)), dma((2, 2)), dma(both + (2,)), dma(both), dma(both), dma(both),
            dma(both + (2,)), dma(both),
        ],
        compiler_params=pltpu.CompilerParams(
            collective_id=0, has_side_effects=True, vmem_limit_bytes=67_043_328 - 8 * shard * probe_count
        ),
    )(near, right_bases[0, 0], left_bases[0, 0], probes, tile_ranks, row_columns)


def shifted(block, axis, distance):
    devices = range(lax.axis_size(axis))
    route = [(i - distance, i) for i in devices if i - distance in devices]
    return lax.ppermute(block, axis, route)


def image_part(operand, right_bases, left_bases, near_tiles, tile_ranks, column_rows, row_columns):
    tile_slots = right_bases.shape[1]
    rank_part = right_bases.shape[2]
    tile_rows = right_bases.shape[3]
    probe_count = operand.shape[1]
    tile_count = lax.axis_size("tile")
    right_flat = right_bases.reshape(tile_slots * rank_part, tile_rows)
    left_flat = left_bases.reshape(tile_slots * rank_part, tile_rows)
    dense_flat = near_tiles.reshape(tile_rows, -1)
    values = jnp.dot(
        right_flat,
        lax.all_gather(operand, "list", axis=0, tiled=True),
        preferred_element_type=jnp.float32,
    )
    rank_level = lax.axis_index("list") * rank_part + lax.iota(jnp.int32, rank_part)
    rank_mask = rank_level[None, :] < tile_ranks[0][:, None]
    coefficients = jnp.where(
        rank_mask[:, :, None], values.reshape(tile_slots, rank_part, probe_count), 0.0
    ).astype(jnp.bfloat16)
    targets = (column_rows[0][None, :] == lax.iota(jnp.int32, tile_count)[:, None]).astype(
        jnp.bfloat16
    )
    outgoing = jnp.einsum(
        "dk,krp->drp", targets, coefficients, preferred_element_type=jnp.float32
    ).astype(jnp.bfloat16)
    sources = (row_columns[0][:, None] == lax.iota(jnp.int32, tile_count)[None, :]).astype(
        jnp.bfloat16
    )
    chosen = jnp.einsum(
        "kj,jrp->krp",
        sources,
        lax.all_to_all(outgoing, "tile", split_axis=0, concat_axis=0, tiled=True),
        preferred_element_type=jnp.float32,
    ).astype(jnp.bfloat16)
    chosen = chosen.reshape(tile_slots * rank_part, -1)
    far_sum = lax.dot_general(
        left_flat, chosen, (((0,), (0,)), ((), ())), preferred_element_type=jnp.float32
    )
    arrived = {}
    for offset in (1, -1):
        arrived[offset] = shifted(operand, "tile", offset)
    stacked = jnp.concatenate([arrived[1], operand, arrived[-1]], axis=0)
    near_sum = jnp.dot(dense_flat, stacked, preferred_element_type=jnp.float32)
    partial_image = near_sum + far_sum
    return lax.psum_scatter(partial_image, "list", scatter_dimension=0, tiled=True)


def local(probes, right_bases, left_bases, near_tiles, tile_ranks, column_rows, row_columns):
    list_count, tile_count = lax.axis_size("list"), lax.axis_size("tile")
    if list_count == 4 and right_bases.shape[1] == 1 and 2 < tile_count <= 8:
        return fused(
            tile_count, probes, right_bases, left_bases, near_tiles, tile_ranks, row_columns
        )
    probe_bf = probes.astype(jnp.bfloat16)
    first_pass = image_part(
        probe_bf, right_bases, left_bases, near_tiles, tile_ranks, column_rows, row_columns
    ).astype(jnp.bfloat16)
    return image_part(
        first_pass, right_bases, left_bases, near_tiles, tile_ranks, column_rows, row_columns
    )


def solution(mesh):
    placed = (
        P(("group", "tile", "list"), None),
        P(("group", "tile"), None, "list", None),
        P(("group", "tile"), None, "list", None),
        P(("group", "tile"), None, None, "list"),
        P(("group", "tile"), None),
        P("tile", None),
        P("tile", None),
    )
    return jax.shard_map(
        local,
        mesh=mesh,
        in_specs=placed,
        out_specs=P(("group", "tile", "list"), None),
        check_vma=False,
    )
```

```python
import functools

import jax
import jax.numpy as jnp
from jax import lax
from jax.experimental import pallas as pl
from jax.experimental.pallas import tpu as pltpu
from jax.sharding import PartitionSpec as P

MESH = pl.DeviceIdType.MESH
BF16 = jnp.bfloat16
F32 = jnp.float32
CHUNKS = 2
FLIPS = ((0, 0), (0, 1), (1, 0), (1, 1))


def fused_kernel(
    tiles, near, right, left, probes, ranks, rows, out,
    near_v, probe_v, right_v, left_v, right_x, left_x, left_n, right_c, left_t, left_tn,
    row_send, row_recv, mix_part, mix_recv, mix,
    w, zbuf, stack, center, kept, osend, orecv, osend2, orecv2, xsend, xrecv, fin,
    pc, prec, cbuf, crecv, sbuf, srecv, sbuf2, srecv2,
    local_sem, send_sem, set_recv, side_recv, z_recv, p_recv, c_recv, s_recv, o_recv, x_recv,
):
    g, t, l = lax.axis_index("group"), lax.axis_index("tile"), lax.axis_index("list")
    x, c = l // 2, l % 2
    rank_part = right.shape[0]
    shard = probes.shape[0]
    width = probes.shape[1] // CHUNKS
    padding = right_c.shape[0] - 4 * rank_part

    def peer(k):
        return (x + FLIPS[k][0]) % 2 * 2 + (c + FLIPS[k][1]) % 2

    def joined(parts):
        rest = [jnp.zeros((padding, parts[0].shape[1]), F32)] if padding else []
        return jnp.concatenate([part.astype(F32) for part in parts] + rest, axis=0)

    loads = [pltpu.make_async_copy(probes, probe_v, local_sem.at[0])]
    for at, s in enumerate((1, 0, 2)):
        place = (2, 0, 1)[at]
        loads.append(
            pltpu.make_async_copy(
                near.at[s], near_v.at[:, :, pl.ds(place * shard, shard)], local_sem.at[1 + at]
            )
        )
    own = pl.ds(pl.multiple_of(l * shard, shard), shard)
    loads.insert(0, pltpu.make_async_copy(right, right_v, local_sem.at[4]))
    loads.insert(2, pltpu.make_async_copy(left, left_v, local_sem.at[5]))
    for load in loads:
        load.start()

    barrier = pltpu.get_barrier_semaphore()
    for k in (1, 2, 3):
        pl.semaphore_signal(barrier, inc=1, device_id=(g, t, peer(k)), device_id_type=MESH)
    for d in range(1, tiles):
        pl.semaphore_signal(barrier, inc=1, device_id=(g, (t + d) % tiles, l), device_id_type=MESH)

    for way, edge in ((0, 0), (1, tiles - 1)):

        @pl.when(t == edge)
        def _():
            zbuf[:, :, way * shard : (way + 1) * shard, :] = jnp.zeros((2, CHUNKS, shard, width), BF16)
            left_n[way] = jnp.zeros(left_n.shape[1:], BF16)
            row_recv[way] = jnp.full(row_recv.shape[1:], -1, jnp.int32)

    row_send[...] = jnp.full(row_send.shape, rows[0, 0], jnp.int32)

    loads[1].wait()
    for ch in range(CHUNKS):
        w[0, ch] = probe_v[:, ch * width : (ch + 1) * width].astype(BF16)
    pl.semaphore_wait(barrier, 3 + tiles - 1)

    sent = []

    def arrive(held, sem):
        pltpu.make_async_copy(held, held, sem).wait()

    def send(src, dst, rsem, tile, lst):
        copy = pltpu.make_async_remote_copy(
            src_ref=src, dst_ref=dst, send_sem=send_sem, recv_sem=rsem,
            device_id=(g, tile, lst), device_id_type=MESH,
        )
        copy.start()
        sent.append(copy)
        return copy

    class Both:
        def __init__(self, src, dst, rsem):
            self.copies = [
                pltpu.make_async_remote_copy(
                    src_ref=src, dst_ref=dst(way), send_sem=send_sem, recv_sem=rsem.at[way],
                    device_id=(g, (t + (1 if way == 0 else tiles - 1)) % tiles, l),
                    device_id_type=MESH,
                )
                for way in range(2)
            ]

        def each(self, act, holds):
            for copy, held in zip(self.copies, holds):

                @pl.when(held)
                def _(copy=copy):
                    act(copy)

        def start(self):
            self.each(lambda copy: copy.start(), (t < tiles - 1, t > 0))
            return self

        def wait_send(self):
            self.each(lambda copy: copy.wait_send(), (t < tiles - 1, t > 0))

        def wait_recv(self):
            self.each(lambda copy: copy.wait_recv(), (t > 0, t < tiles - 1))

    flying = {}

    def z_start(p, ch):
        flying["z", p, ch] = Both(
            w.at[p, ch], lambda way: zbuf.at[p, ch, pl.ds(way * shard, shard)],
            z_recv.at[p, ch],
        ).start()
        sent.append(flying["z", p, ch])

    order = [((x + 1) % 2) * 2 + (1 - c), x * 2 + (1 - c), ((x + 1) % 2) * 2 + c, x * 2 + c]

    def stage_pc(p, ch):
        values = jnp.dot(right_c[...], w[p, ch], preferred_element_type=F32)
        for k in range(4):
            pc[p, ch, k] = values[k * rank_part : (k + 1) * rank_part].astype(BF16)
        for k in (1, 2, 3):
            send(pc.at[p, ch, peer(k)], prec.at[p, ch, k - 1], p_recv.at[p, ch], t, peer(k))

    def stage_center(ch):
        for at in range(4):
            center[ch, at] = jnp.dot(
                near_v[order[at], :, 2 * shard : 3 * shard], w[0, ch], preferred_element_type=F32
            )

    def stage_b(p, ch, more=None):
        arrive(prec.at[p, ch], p_recv.at[p, ch])
        values = sum(prec[p, ch, k].astype(F32) for k in range(3)) + pc[p, ch, l].astype(F32)
        if more is not None:
            values = values + more
        level = l * rank_part + lax.broadcasted_iota(jnp.int32, values.shape, 0)
        cbuf[p, ch] = jnp.where(level < ranks[0, 0], values, 0.0).astype(BF16)
        for d in range(1, tiles):
            send(cbuf.at[p, ch], crecv.at[p, ch, d - 1], c_recv.at[p, ch], (t + d) % tiles, l)

    def row_block(p, ch, at):
        if p == 0:
            return center[ch, at] + jnp.dot(
                near_v[order[at], :, 0 : 2 * shard], zbuf[0, ch], preferred_element_type=F32
            )
        return jnp.dot(near_v[order[at]], stack[ch], preferred_element_type=F32)

    def stage_c(p, ch, between=None):
        for at in range(4):
            if at == 2 and between is not None:
                between()
            value = row_block(p, ch, at)
            if at < 2:
                out_of, into = (osend, orecv) if p == 0 else (osend2, orecv2)
                out_of[ch, at] = value.astype(out_of.dtype)
                flying["o", p, ch, at] = send(
                    out_of.at[ch, at], into.at[ch, at], o_recv.at[p, ch, at], t, peer(1)
                )
            else:
                kept[ch, at - 2] = value

    def stage_d(p, ch):
        flying["o", p, ch, 0].wait_recv()
        into = orecv if p == 0 else orecv2
        xsend[p, ch] = (kept[ch, 0] + into[ch, 0].astype(F32)).astype(BF16)
        flying["x", p, ch] = send(
            xsend.at[p, ch], xrecv.at[p, ch], x_recv.at[p, ch], t, peer(2)
        )
        flying["o", p, ch, 1].wait_recv()
        fin[ch] = kept[ch, 1] + into[ch, 1].astype(F32)

    def stage_n(ch):
        flying["x", 0, ch].wait_recv()
        value = fin[ch] + xrecv[0, ch].astype(F32)
        fin[ch] = value
        w[1, ch] = value.astype(BF16)
        z_start(1, ch)
        stage_pc(1, ch)

    def stage_e(p, ch):
        arrive(crecv.at[p, ch], c_recv.at[p, ch])
        blocks = [cbuf[p, ch].astype(F32)]
        for d in range(1, tiles):
            blocks.append(crecv[p, ch, d - 1].astype(F32))

        def chosen(wanted):
            value = jnp.zeros(blocks[0].shape, F32)
            for d in range(tiles):
                value = jnp.where(wanted == (t + tiles - d) % tiles, blocks[d], value)
            return value.astype(BF16)

        if p == 0:
            sbuf[ch, 0] = chosen(rows[0, 0])
            for way in range(2):
                sbuf[ch, 1 + way] = chosen(row_recv[way, 0:1, 0:width])
            source, held = sbuf.at[ch], srecv.at[ch, l]
        else:
            sbuf2[ch] = chosen(rows[0, 0])
            source, held = sbuf2.at[ch], srecv2.at[ch, l]
        for k in (1, 2, 3):
            send(source, held, s_recv.at[p, ch], t, peer(k))
        if p == 0:
            srecv[ch, l] = sbuf[ch]
        else:
            srecv2[ch, l] = sbuf2[ch]

    chosen_of = {}

    def stage_g(ch):
        arrive(srecv.at[ch, pl.ds(0, 3)], s_recv.at[0, ch])
        of = [joined([srecv[ch, k, at] for k in range(4)]).astype(BF16) for at in range(3)]
        stage_b(1, ch, jnp.dot(mix[...], of[0], preferred_element_type=F32))
        chosen_of[ch] = of

    def stage_w(ch):
        of = chosen_of[ch]
        far = jnp.dot(left_t[...], of[0], preferred_element_type=F32)
        stack[ch, 2 * shard : 3 * shard] = (fin[ch] + far).astype(BF16)
        flying["z", 1, ch].wait_recv()
        for way in range(2):
            far = jnp.dot(left_tn[way], of[1 + way], preferred_element_type=F32)
            part = slice(way * shard, (way + 1) * shard)
            stack[ch, part] = (zbuf[1, ch, part].astype(F32) + far).astype(BF16)

    def stage_f(ch):
        arrive(srecv2.at[ch, pl.ds(0, 3)], s_recv.at[1, ch])
        coefficients = joined([srecv2[ch, k] for k in range(4)]).astype(BF16)
        far = fin[ch] + jnp.dot(left_t[...], coefficients, preferred_element_type=F32)
        flying["x", 1, ch].wait_recv()
        out[:, ch * width : (ch + 1) * width] = far + xrecv[1, ch].astype(F32)

    def bases(source, held, at):
        for k in (1, 2, 3):
            columns = pl.ds(pl.multiple_of(peer(k) * shard, shard), shard)
            send(source.at[:, columns], held.at[l], set_recv.at[at], t, peer(k))
        held[l] = source[:, own]

    loads[0].wait()
    bases(right_v, right_x, 0)
    for ch in range(CHUNKS):
        z_start(0, ch)
    loads[2].wait()
    bases(left_v, left_x, 1)
    row_copies = Both(row_send, lambda way: row_recv.at[way], side_recv.at[0]).start()
    sent.append(row_copies)
    loads[3].wait()
    for ch in range(CHUNKS):
        stage_center(ch)
    arrive(right_x.at[pl.ds(0, 3)], set_recv.at[0])
    right_c[...] = joined([right_x[k] for k in range(4)]).astype(BF16)
    for ch in range(CHUNKS):
        stage_pc(0, ch)
    arrive(left_x.at[pl.ds(0, 3)], set_recv.at[1])
    beside = Both(left_x, lambda way: left_n.at[way], side_recv.at[1]).start()
    sent.append(beside)
    left_t[...] = joined([left_x[k] for k in range(4)]).T.astype(BF16)
    loads[4].wait()
    loads[5].wait()
    for ch in range(CHUNKS):
        flying["z", 0, ch].wait_recv()
        stage_c(0, ch)
    stage_d(0, 0)
    for ch in range(CHUNKS):
        stage_b(0, ch)
    stage_d(0, 1)

    part = jnp.dot(right_c[...], left_t[...], preferred_element_type=F32)
    for k in range(4):
        mix_part[k] = part[k * rank_part : (k + 1) * rank_part]
    for k in (1, 2, 3):
        send(mix_part.at[peer(k)], mix_recv.at[k - 1], set_recv.at[2], t, peer(k))
    beside.wait_recv()
    row_copies.wait_recv()
    for way in range(2):
        left_tn[way] = joined([left_n[way, k] for k in range(4)]).T.astype(BF16)

    stage_n(0)
    stage_e(0, 0)
    stage_n(1)
    stage_e(0, 1)
    arrive(mix_recv, set_recv.at[2])
    mix[...] = (mix_part[l] + mix_recv[0] + mix_recv[1] + mix_recv[2]).astype(BF16)
    stage_g(0)
    stage_w(0)
    stage_c(1, 0, lambda: stage_g(1))
    stage_w(1)
    stage_d(1, 0)
    stage_c(1, 1)
    stage_e(1, 0)
    stage_d(1, 1)
    stage_e(1, 1)
    for ch in range(CHUNKS):
        stage_f(ch)

    for copy in sent:
        copy.wait_send()


def fused(tiles, probes, right_bases, left_bases, near_tiles, tile_ranks, row_columns):
    rank_part = right_bases.shape[2]
    shard, probe_count = probes.shape
    width = probe_count // CHUNKS
    near = near_tiles[0].transpose(1, 0, 2).reshape(3, 4, shard, shard)
    both = (2, CHUNKS)
    full = -(-4 * rank_part // 128) * 128
    any_spec = pl.BlockSpec(memory_space=pltpu.HBM)
    smem_spec = pl.BlockSpec(memory_space=pltpu.SMEM)
    dma = pltpu.SemaphoreType.DMA
    return pl.pallas_call(
        functools.partial(fused_kernel, tiles),
        out_shape=pltpu.VMEM((shard, probe_count), F32),
        in_specs=[any_spec] * 4 + [smem_spec] * 2,
        out_specs=pl.BlockSpec(memory_space=pltpu.VMEM),
        scratch_shapes=[
            pltpu.VMEM((4, shard, 3 * shard), BF16),
            pltpu.VMEM((shard, probe_count), F32),
            pltpu.VMEM((rank_part, 4 * shard), BF16),
            pltpu.VMEM((rank_part, 4 * shard), BF16),
            pltpu.VMEM((4, rank_part, shard), BF16),
            pltpu.VMEM((4, rank_part, shard), BF16),
            pltpu.VMEM((2, 4, rank_part, shard), BF16),
            pltpu.VMEM((full, shard), BF16),
            pltpu.VMEM((shard, full), BF16),
            pltpu.VMEM((2, shard, full), BF16),
            pltpu.VMEM((8, width), jnp.int32),
            pltpu.VMEM((2, 8, width), jnp.int32),
            pltpu.VMEM((4, rank_part, full), F32),
            pltpu.VMEM((3, rank_part, full), F32),
            pltpu.VMEM((rank_part, full), BF16),
            pltpu.VMEM(both + (shard, width), BF16),
            pltpu.VMEM(both + (2 * shard, width), BF16),
            pltpu.VMEM((CHUNKS, 3 * shard, width), BF16),
            pltpu.VMEM((CHUNKS, 4, shard, width), F32),
            pltpu.VMEM((CHUNKS, 2, shard, width), F32),
            pltpu.VMEM((CHUNKS, 2, shard, width), F32),
            pltpu.VMEM((CHUNKS, 2, shard, width), F32),
            pltpu.VMEM((CHUNKS, 2, shard, width), BF16),
            pltpu.VMEM((CHUNKS, 2, shard, width), BF16),
            pltpu.VMEM(both + (shard, width), BF16),
            pltpu.VMEM(both + (shard, width), BF16),
            pltpu.VMEM((CHUNKS, shard, width), F32),
            pltpu.VMEM(both + (4, rank_part, width), BF16),
            pltpu.VMEM(both + (3, rank_part, width), BF16),
            pltpu.VMEM(both + (rank_part, width), BF16),
            pltpu.VMEM(both + (tiles - 1, rank_part, width), BF16),
            pltpu.VMEM((CHUNKS, 3, rank_part, width), BF16),
            pltpu.VMEM((CHUNKS, 4, 3, rank_part, width), BF16),
            pltpu.VMEM((CHUNKS, rank_part, width), BF16),
            pltpu.VMEM((CHUNKS, 4, rank_part, width), BF16),
            dma((6,)), dma, dma((3,)), dma((2, 2)), dma(both + (2,)), dma(both), dma(both), dma(both),
            dma(both + (2,)), dma(both),
        ],
        compiler_params=pltpu.CompilerParams(
            collective_id=0, has_side_effects=True, vmem_limit_bytes=67_043_328 - 8 * shard * probe_count
        ),
    )(near, right_bases[0, 0], left_bases[0, 0], probes, tile_ranks, row_columns)


def shifted(block, axis, distance):
    devices = range(lax.axis_size(axis))
    route = [(i - distance, i) for i in devices if i - distance in devices]
    return lax.ppermute(block, axis, route)


def image_part(operand, right_bases, left_bases, near_tiles, tile_ranks, column_rows, row_columns):
    tile_slots = right_bases.shape[1]
    rank_part = right_bases.shape[2]
    tile_rows = right_bases.shape[3]
    probe_count = operand.shape[1]
    tile_count = lax.axis_size("tile")
    right_flat = right_bases.reshape(tile_slots * rank_part, tile_rows)
    left_flat = left_bases.reshape(tile_slots * rank_part, tile_rows)
    dense_flat = near_tiles.reshape(tile_rows, -1)
    values = jnp.dot(
        right_flat,
        lax.all_gather(operand, "list", axis=0, tiled=True),
        preferred_element_type=jnp.float32,
    )
    rank_level = lax.axis_index("list") * rank_part + lax.iota(jnp.int32, rank_part)
    rank_mask = rank_level[None, :] < tile_ranks[0][:, None]
    coefficients = jnp.where(
        rank_mask[:, :, None], values.reshape(tile_slots, rank_part, probe_count), 0.0
    ).astype(jnp.bfloat16)
    targets = (column_rows[0][None, :] == lax.iota(jnp.int32, tile_count)[:, None]).astype(
        jnp.bfloat16
    )
    outgoing = jnp.einsum(
        "dk,krp->drp", targets, coefficients, preferred_element_type=jnp.float32
    ).astype(jnp.bfloat16)
    sources = (row_columns[0][:, None] == lax.iota(jnp.int32, tile_count)[None, :]).astype(
        jnp.bfloat16
    )
    chosen = jnp.einsum(
        "kj,jrp->krp",
        sources,
        lax.all_to_all(outgoing, "tile", split_axis=0, concat_axis=0, tiled=True),
        preferred_element_type=jnp.float32,
    ).astype(jnp.bfloat16)
    chosen = chosen.reshape(tile_slots * rank_part, -1)
    far_sum = lax.dot_general(
        left_flat, chosen, (((0,), (0,)), ((), ())), preferred_element_type=jnp.float32
    )
    arrived = {}
    for offset in (1, -1):
        arrived[offset] = shifted(operand, "tile", offset)
    stacked = jnp.concatenate([arrived[1], operand, arrived[-1]], axis=0)
    near_sum = jnp.dot(dense_flat, stacked, preferred_element_type=jnp.float32)
    partial_image = near_sum + far_sum
    return lax.psum_scatter(partial_image, "list", scatter_dimension=0, tiled=True)


def local(probes, right_bases, left_bases, near_tiles, tile_ranks, column_rows, row_columns):
    list_count, tile_count = lax.axis_size("list"), lax.axis_size("tile")
    if list_count == 4 and right_bases.shape[1] == 1 and 2 < tile_count <= 8:
        return fused(
            tile_count, probes, right_bases, left_bases, near_tiles, tile_ranks, row_columns
        )
    probe_bf = probes.astype(jnp.bfloat16)
    first_pass = image_part(
        probe_bf, right_bases, left_bases, near_tiles, tile_ranks, column_rows, row_columns
    ).astype(jnp.bfloat16)
    return image_part(
        first_pass, right_bases, left_bases, near_tiles, tile_ranks, column_rows, row_columns
    )


def solution(mesh):
    placed = (
        P(("group", "tile", "list"), None),
        P(("group", "tile"), None, "list", None),
        P(("group", "tile"), None, "list", None),
        P(("group", "tile"), None, None, "list"),
        P(("group", "tile"), None),
        P("tile", None),
        P("tile", None),
    )
    return jax.shard_map(
        local,
        mesh=mesh,
        in_specs=placed,
        out_specs=P(("group", "tile", "list"), None),
        check_vma=False,
    )
```
